32 devices in a mesh: row: 2 (over x), col: 16 (over z, y, core).
Axes of the slice: x: 2, y: 2, z: 4, core: 2. Of those that a mesh axis runs over, the one named last changes fastest.
Arguments:
- diagonal_tile: float32 [512, 512], P('row'), may hold values from -1 to 8, as said below
- panel: float32 [2048, 512], P(('row', 'col')), may hold values from -2.5 to 2.5
- trailing: bfloat16 [2048, 2048], P('col', 'row'), may hold values from -6 to 6
Outputs:
- factor_panel: float32 [2048, 512], P(('row', 'col'))
- updated: bfloat16 [2048, 2048], P('col', 'row')
The draws below stay inside these ranges and needn't reach their ends.
Inputs may be any that keep to these rules, and one draw needn't show every extreme that they name: `diagonal_tile`: symmetric, and every eigenvalue is at least 1.
All inputs are finite; a program needn't handle non-finite values.
Results may differ from the reference program's by a relative error of at most 0.0085.
Values may be sent and summed in bfloat16 or wider, within the bound.
A program may use at most 64 MiB of HBM per device.

```python
import jax
import jax.numpy as jnp
from jax import lax

B = 512
COLS_DEV = 128
N = 2048
CH = 64
N_ROW = 2
N_COL = 16


def draw_diagonal_tile(key, part):
    key_factor = jax.random.fold_in(key, 11)
    key_shift = jax.random.fold_in(key, 12)
    factor = jax.random.normal(key_factor, (B, B), jnp.float32)
    diag_shift = jax.random.uniform(key_shift, (B,), jnp.float32, 1.0, 2.0)
    gram_matrix = jnp.dot(factor, factor.T, precision=lax.Precision.HIGHEST) / B
    common_part = jnp.full((B, B), 4.0, jnp.float32)
    return gram_matrix + jnp.diag(diag_shift) + common_part


def level_of(stream_key, extent, split, low, top_value):
    gain = 1.0
    for position, blocks in split:
        steps = jax.random.uniform(jax.random.fold_in(jax.random.fold_in(stream_key, 6), position), (blocks,), jnp.float32, low / len(split), top_value / len(split))
        gain = gain * jnp.repeat(jnp.exp(steps), extent[position] // blocks).reshape((-1,) + (1,) * (len(extent) - 1 - position))
    return gain


def gaussian(own_key, shape, spread, reach, shards=(), held_as=jnp.bfloat16):
    array = spread * jax.random.normal(own_key, shape, jnp.float32)
    if shards:
        array = array * level_of(own_key, shape, shards, -0.22, 0.18)
    return jnp.clip(array, -reach, reach).astype(held_as)


def setup_inputs(seed: int = 0) -> dict:
    seeds = jax.random.split(jax.random.key(seed), 4)
    return {
        "diagonal_tile": draw_diagonal_tile(jax.random.fold_in(seeds[3], 71), 0),
        "panel": gaussian(seeds[1], (N, B), 0.3, 2.5, ((0, 32),), jnp.float32),
        "trailing": gaussian(seeds[2], (N, N), 1.0, 6.0, ((0, 16), (1, 2))),
    }


def reference(diagonal_tile, panel, trailing):
    diag_factor = jnp.linalg.cholesky(diagonal_tile)
    factor_panel = jax.scipy.linalg.solve_triangular(diag_factor, panel.T, lower=True).T
    low_panel = factor_panel.astype(jnp.bfloat16)
    column_panel = low_panel.reshape(N_ROW, N_COL, CH, B).transpose(1, 0, 2, 3).reshape(N_COL, COLS_DEV, B)

    def one_block(operands):
        trail_block, column_block = operands
        outer_term = lax.dot_general(column_block.astype(jnp.float32), low_panel.astype(jnp.float32), (((1,), (1,)), ((), ())), preferred_element_type=jnp.float32)
        return (trail_block.astype(jnp.float32) - outer_term).astype(jnp.bfloat16)
    updated = lax.map(one_block, (trailing.reshape(N_COL, COLS_DEV, N), column_panel)).reshape(N, N)
    return (factor_panel, updated)
```

```python
import functools

import jax
import jax.numpy as jnp
from jax import lax
from jax.experimental import pallas as pl
from jax.experimental.pallas import tpu as pltpu
from jax.sharding import PartitionSpec as P

F32 = jnp.float32
BF16 = jnp.bfloat16
NB = 128
SUB = 8
BASE = 16
MESH = pl.DeviceIdType.MESH


def split2(x):
    hi = x.astype(BF16)
    return hi, (x - hi.astype(F32)).astype(BF16)


def dot3(a, b, dims):
    dims = (dims, ((), ()))
    a_hi, a_lo = split2(a)
    b_hi, b_lo = split2(b)
    dot = functools.partial(lax.dot_general, dimension_numbers=dims, preferred_element_type=F32)
    return dot(a_hi, b_hi) + (dot(a_hi, b_lo) + dot(a_lo, b_hi))


def dot_nt(a, b):
    return dot3(a, b, ((1,), (1,)))


def dot_nn(a, b):
    return dot3(a, b, ((1,), (0,)))


def row_of(x, s):
    return jnp.broadcast_to(x[s : s + 1, :], x.shape)


def lower_inverse(a):
    halves = BASE // SUB
    eye = (
        lax.broadcasted_iota(jnp.int32, (NB, NB), 0) == lax.broadcasted_iota(jnp.int32, (NB, NB), 1)
    ).astype(F32)
    iota = lax.broadcasted_iota(jnp.int32, (SUB, NB), 0)
    chunks = [
        (a[s : s + BASE, :], eye[s : s + BASE, :]) for s in range(0, NB, BASE)
    ]
    inverse_rows = []
    for kb in range(NB // BASE):
        cur = [
            [part[h * SUB : (h + 1) * SUB, :] for part in chunks[kb]] for h in range(halves)
        ]
        first = kb * BASE
        cols = [
            [
                jnp.broadcast_to(cur[h][0][:, first + c : first + c + 1], (SUB, NB))
                for h in range(halves)
            ]
            for c in range(BASE)
        ]
        scale = [jnp.zeros((SUB, NB), F32) for _ in range(halves)]
        for k in range(BASE):
            hk, sk = k // SUB, k % SUB
            root = lax.rsqrt(row_of(cols[k][hk], sk))
            inv = root * root
            scale[hk] = jnp.where(iota == sk, root, scale[hk])
            mult = {h: cols[k][h] * inv for h in range(hk, halves)}
            mult[hk] = jnp.where(iota > sk, mult[hk], 0.0)
            for c in range(k + 1, BASE):
                row = row_of(cols[c][hk], sk)
                for h in range(hk, halves):
                    cols[c][h] = cols[c][h] - mult[h] * row
            for part in range(2):
                row = row_of(cur[hk][part], sk)
                for h in range(hk, halves):
                    cur[h][part] = cur[h][part] - mult[h] * row
        done = [
            jnp.concatenate([cur[h][part] * scale[h] for h in range(halves)], axis=0)
            for part in range(2)
        ]
        inverse_rows.append(done[1])
        if kb + 1 < NB // BASE:
            pieces = []
            for part in range(2):
                hi = done[part].astype(BF16).astype(F32)
                pieces.append((hi, done[part] - hi))
            left = jnp.concatenate([pieces[0][0], pieces[0][0], pieces[0][1]], axis=0)
            left = left.T.astype(BF16)
            right = jnp.concatenate(
                [
                    jnp.concatenate([hi, lo, hi], axis=0) for hi, lo in pieces
                ],
                axis=1,
            ).astype(BF16)
            start = (kb + 1) * BASE
            change = lax.dot_general(
                left[start:, :], right, (((1,), (0,)), ((), ())), preferred_element_type=F32
            )
            for j in range(kb + 1, NB // BASE):
                at = j * BASE - start
                chunks[j] = tuple(
                    chunks[j][part] - change[at : at + BASE, part * NB : (part + 1) * NB]
                    for part in range(2)
                )
    return jnp.concatenate(inverse_rows, axis=0)


def kernel(
    n_row, n_col,
    tile_ref, panel_ref, trailing_ref,
    factor_ref, updated_ref,
    tile, rows, raw,
    tile_send, tile_recv, rows_send, rows_recv, raw_send, raw_recv,
):
    r = lax.axis_index("row")
    c = lax.axis_index("col")
    order = tile_ref.shape[1]
    blocks = order // NB
    per_dev = tile_ref.shape[0] // NB
    ch = panel_ref.shape[0]

    def row_peer(d):
        return (lax.rem(r + d, n_row), c)

    def col_peer(d):
        return (r, lax.rem(c + d, n_col))

    barrier = pltpu.get_barrier_semaphore()
    for d in range(1, n_row):
        pl.semaphore_signal(barrier, inc=1, device_id=row_peer(d), device_id_type=MESH)

    @pl.loop(1, n_col)
    def _(d):
        pl.semaphore_signal(barrier, inc=1, device_id=col_peer(d), device_id_type=MESH)

    own_raw = pl.ds(pl.multiple_of(c * ch, ch), ch)
    own_rows = pl.ds(pl.multiple_of(r * ch, ch), ch)
    raw[own_raw, :] = panel_ref[...].astype(BF16)
    rows[own_rows, :] = panel_ref[...]
    pl.semaphore_wait(barrier, n_row - 1 + n_col - 1)

    def tile_copy(i, d):
        source = pl.ds((i % per_dev) * NB, NB)
        cols = pl.ds(0, (i + 1) * NB)
        return pltpu.make_async_remote_copy(
            src_ref=tile_ref.at[source, cols],
            dst_ref=tile.at[pl.ds(i * NB, NB), cols],
            send_sem=tile_send.at[i, d - 1],
            recv_sem=tile_recv.at[i],
            device_id=row_peer(d),
            device_id_type=MESH,
        )

    def rows_copy(d):
        return pltpu.make_async_remote_copy(
            src_ref=panel_ref,
            dst_ref=rows.at[own_rows, :],
            send_sem=rows_send.at[d - 1],
            recv_sem=rows_recv.at[d - 1],
            device_id=row_peer(d),
            device_id_type=MESH,
        )

    def raw_copy(d):
        return pltpu.make_async_remote_copy(
            src_ref=raw.at[own_raw, :],
            dst_ref=raw.at[own_raw, :],
            send_sem=raw_send.at[d - 1],
            recv_sem=raw_recv.at[d - 1],
            device_id=col_peer(d),
            device_id_type=MESH,
        )

    for i in range(blocks):
        @pl.when(r == i // per_dev)
        def _():
            for d in range(1, n_row):
                tile_copy(i, d).start()
            here = (i % per_dev) * NB
            tile[i * NB : (i + 1) * NB, :] = tile_ref[here : here + NB, :]

    for d in range(1, n_row):
        rows_copy(d).start()

    @pl.loop(1, n_col)
    def _(d):
        raw_copy(d).start()

    def wait_tile(i):
        @pl.when(r != i // per_dev)
        def _():
            tile_copy(i, 1).wait_recv()

    def sl(i):
        return slice(i * NB, (i + 1) * NB)

    inverses = []
    for j in range(blocks):
        if j == 0:
            wait_tile(0)
        inv = lower_inverse(tile[sl(j), sl(j)])
        inverses.append(inv)
        if j == 0:
            for i in range(1, blocks):
                wait_tile(i)
            for d in range(1, n_row):
                rows_copy(d).wait_recv()
        solved = dot_nt(rows[:, sl(j)], inv)
        rows[:, sl(j)] = solved
        if j + 1 < blocks:
            lower = dot_nt(tile[(j + 1) * NB :, sl(j)], inv)
            tile[(j + 1) * NB :, sl(j)] = lower
            for k in range(j + 1, blocks):
                at = (k - j - 1) * NB
                pivot = lower[at : at + NB, :]
                tile[k * NB :, sl(k)] = tile[k * NB :, sl(k)] - dot_nt(lower[at:, :], pivot)
                rows[:, sl(k)] = rows[:, sl(k)] - dot_nt(solved, pivot)

    factor_ref[...] = rows[own_rows, :]
    weights = [None] * blocks
    for j in reversed(range(blocks)):
        value = rows[:, sl(j)]
        for i in range(j + 1, blocks):
            value = value - dot_nn(weights[i], tile[sl(i), sl(j)])
        weights[j] = dot_nn(value, inverses[j])
    weight = jnp.concatenate([w.astype(BF16) for w in weights], axis=1)

    @pl.loop(1, n_col)
    def _(d):
        raw_copy(d).wait_recv()

    wide = trailing_ref.shape[1]
    step = min(512, wide)
    for s in range(0, wide, step):
        term = lax.dot_general(
            weight, raw[s : s + step, :], (((1,), (1,)), ((), ())), preferred_element_type=F32
        )
        updated_ref[:, s : s + step] = (
            trailing_ref[:, s : s + step].astype(F32) - term
        ).astype(BF16)

    for i in range(blocks):
        @pl.when(r == i // per_dev)
        def _():
            for d in range(1, n_row):
                tile_copy(i, d).wait_send()
    for d in range(1, n_row):
        rows_copy(d).wait_send()

    @pl.loop(1, n_col)
    def _(d):
        raw_copy(d).wait_send()


def per_device(n_row, n_col, diagonal_tile, panel, trailing):
    order = diagonal_tile.shape[1]
    ch = panel.shape[0]
    dma = pltpu.SemaphoreType.DMA
    vmem = pl.BlockSpec(memory_space=pltpu.VMEM)
    return pl.pallas_call(
        functools.partial(kernel, n_row, n_col),
        out_shape=(
            jax.ShapeDtypeStruct(panel.shape, F32),
            jax.ShapeDtypeStruct(trailing.shape, BF16),
        ),
        in_specs=[vmem] * 3,
        out_specs=(vmem, vmem),
        scratch_shapes=[
            pltpu.VMEM((order, order), F32),
            pltpu.VMEM((n_row * ch, order), F32),
            pltpu.VMEM((n_col * ch, order), BF16),
            dma((order // NB, n_row - 1)),
            dma((order // NB,)),
            dma((n_row - 1,)),
            dma((n_row - 1,)),
            dma((n_col - 1,)),
            dma((n_col - 1,)),
        ],
        compiler_params=pltpu.CompilerParams(
            collective_id=0, has_side_effects=True, vmem_limit_bytes=48 * 1024 * 1024
        ),
    )(diagonal_tile, panel, trailing)


def solution(mesh):
    return jax.shard_map(
        functools.partial(per_device, mesh.shape["row"], mesh.shape["col"]),
        mesh=mesh,
        in_specs=(P("row", None), P(("row", "col"), None), P("col", "row")),
        out_specs=(P(("row", "col"), None), P("col", "row")),
        check_vma=False,
    )
```

```python
import functools

import jax
import jax.numpy as jnp
from jax import lax
from jax.experimental import pallas as pl
from jax.experimental.pallas import tpu as pltpu
from jax.sharding import PartitionSpec as P

F32 = jnp.float32
BF16 = jnp.bfloat16
NB = 128
SUB = 8
BASE = 32
MESH = pl.DeviceIdType.MESH


def split2(x):
    hi = x.astype(BF16)
    return hi, (x - hi.astype(F32)).astype(BF16)


def dot3(a, b, dims):
    dims = (dims, ((), ()))
    a_hi, a_lo = split2(a)
    b_hi, b_lo = split2(b)
    dot = functools.partial(lax.dot_general, dimension_numbers=dims, preferred_element_type=F32)
    return dot(a_hi, b_hi) + (dot(a_hi, b_lo) + dot(a_lo, b_hi))


def dot_nt(a, b):
    return dot3(a, b, ((1,), (1,)))


def dot_nn(a, b):
    return dot3(a, b, ((1,), (0,)))


def row_of(x, s):
    return jnp.broadcast_to(x[s : s + 1, :], x.shape)


def lower_inverse(a, zero):
    halves = BASE // SUB
    eye = (
        lax.broadcasted_iota(jnp.int32, (NB, NB), 0) == lax.broadcasted_iota(jnp.int32, (NB, NB), 1)
    ).astype(F32)
    iota = lax.broadcasted_iota(jnp.int32, (SUB, NB), 0)
    chunks = [(a[s : s + BASE, :], eye[s : s + BASE, :]) for s in range(0, NB, BASE)]
    inverse_rows = []
    for kb in range(NB // BASE):
        cur = [
            [part[h * SUB : (h + 1) * SUB, :] for part in chunks[kb]] for h in range(halves)
        ]
        first = kb * BASE
        last = kb + 1 == NB // BASE
        parts = (1,) if last else (0, 1)
        cols = [
            {
                h: jnp.broadcast_to(cur[h][0][:, first + c : first + c + 1], (SUB, NB)) + zero
                for h in range(c // SUB, halves)
            }
            for c in range(BASE)
        ]
        scale = [jnp.zeros((SUB, NB), F32) for _ in range(halves)]
        pivot = row_of(cols[0][0], 0)
        for k in range(BASE):
            hk, sk = k // SUB, k % SUB
            root = lax.rsqrt(pivot)
            scale[hk] = jnp.where(iota == sk, root, scale[hk])
            if k + 1 < BASE:
                hn, sn = (k + 1) // SUB, (k + 1) % SUB
                ahead = root * row_of(cols[k][hn], sn)
                pivot = row_of(cols[k + 1][hn], sn) - ahead * ahead
            inv = root * root
            mult = {h: cols[k][h] * inv for h in range(hk, halves)}
            mult[hk] = jnp.where(iota > sk, mult[hk], 0.0)
            for c in range(k + 1, BASE):
                row = row_of(cols[k][c // SUB], c % SUB)
                for h in range(c // SUB, halves):
                    cols[c][h] = cols[c][h] - mult[h] * row
            for part in parts:
                row = row_of(cur[hk][part], sk)
                for h in range(hk, halves):
                    cur[h][part] = cur[h][part] - mult[h] * row
        done = [
            jnp.concatenate([cur[h][part] * scale[h] for h in range(halves)], axis=0)
            for part in range(2)
        ]
        inverse_rows.append(done[1])
        if not last:
            pieces = []
            for part in range(2):
                hi = done[part].astype(BF16).astype(F32)
                pieces.append((hi, done[part] - hi))
            left = jnp.concatenate([pieces[0][0], pieces[0][0], pieces[0][1]], axis=0)
            left = left.T.astype(BF16)
            right = jnp.concatenate(
                [jnp.concatenate([hi, lo, hi], axis=0) for hi, lo in pieces], axis=1
            ).astype(BF16)
            start = (kb + 1) * BASE
            change = lax.dot_general(
                left[start:, :], right, (((1,), (0,)), ((), ())), preferred_element_type=F32
            )
            for j in range(kb + 1, NB // BASE):
                at = j * BASE - start
                chunks[j] = tuple(
                    chunks[j][part] - change[at : at + BASE, part * NB : (part + 1) * NB]
                    for part in range(2)
                )
    return jnp.concatenate(inverse_rows, axis=0)


def kernel(
    n_row, n_col,
    tile_ref, panel_ref, trailing_ref,
    factor_ref, updated_ref,
    tile, rows, raw, trail,
    tile_local, panel_local, trail_local,
    tile_send, tile_recv, rows_send, rows_recv, raw_send, raw_recv, pass_send, pass_recv,
):
    r = lax.axis_index("row")
    c = lax.axis_index("col")
    order = tile_ref.shape[1]
    blocks = order // NB
    per_dev = tile_ref.shape[0] // NB
    ch = panel_ref.shape[0]

    def row_peer(d):
        return (lax.rem(r + d, n_row), c)

    half = n_col // 2
    sibling = (r, c + 1 - 2 * lax.rem(c, 2))

    def col_peer(d):
        return (r, lax.rem(c + 2 * d, n_col))

    barrier = pltpu.get_barrier_semaphore()
    for d in range(1, n_row):
        pl.semaphore_signal(barrier, inc=1, device_id=row_peer(d), device_id_type=MESH)

    pl.semaphore_signal(barrier, inc=1, device_id=sibling, device_id_type=MESH)

    @pl.loop(1, half)
    def _(d):
        pl.semaphore_signal(barrier, inc=1, device_id=col_peer(d), device_id_type=MESH)

    own_raw = pl.ds(pl.multiple_of(c * ch, ch), ch)
    own_rows = pl.ds(pl.multiple_of(r * ch, ch), ch)
    panel_in = pltpu.make_async_copy(panel_ref, rows.at[own_rows, :], panel_local)
    panel_in.start()

    def tile_in(i):
        return pltpu.make_async_copy(
            tile_ref.at[pl.ds((i % per_dev) * NB, NB), :],
            tile.at[pl.ds(i * NB, NB), :],
            tile_local.at[i],
        )

    for i in range(blocks):
        @pl.when(r == i // per_dev)
        def _():
            tile_in(i).start()

    trail_in = pltpu.make_async_copy(trailing_ref, trail, trail_local)
    trail_in.start()
    panel_in.wait()
    raw[own_raw, :] = rows[own_rows, :].astype(BF16)
    pl.semaphore_wait(barrier, n_row - 1 + half)

    def tile_copy(i, d, target=None):
        source = pl.ds((i % per_dev) * NB, NB)
        left = per_dev if target == 0 else 0
        cols = pl.ds(left * NB, (i + 1 - left) * NB)
        return pltpu.make_async_remote_copy(
            src_ref=tile_ref.at[source, cols],
            dst_ref=tile.at[pl.ds(i * NB, NB), cols],
            send_sem=tile_send.at[i, d - 1],
            recv_sem=tile_recv.at[i],
            device_id=row_peer(d),
            device_id_type=MESH,
        )

    def rows_copy(d):
        return pltpu.make_async_remote_copy(
            src_ref=panel_ref,
            dst_ref=rows.at[own_rows, :],
            send_sem=rows_send.at[d - 1],
            recv_sem=rows_recv.at[d - 1],
            device_id=row_peer(d),
            device_id_type=MESH,
        )

    def raw_copy(d):
        return pltpu.make_async_remote_copy(
            src_ref=raw.at[own_raw, :],
            dst_ref=raw.at[own_raw, :],
            send_sem=raw_send.at[d - 1],
            recv_sem=raw_recv.at[d - 1],
            device_id=col_peer(d),
            device_id_type=MESH,
        )

    for i in range(blocks):
        @pl.when(r == i // per_dev)
        def _():
            for d in range(1, n_row):
                tile_copy(i, d, (i // per_dev + d) % n_row).start()

    for d in range(1, n_row):
        rows_copy(d).start()

    def pass_copy(d):
        slot = pl.ds(pl.multiple_of(lax.rem(c + n_col - 2 * d, n_col) * ch, ch), ch)
        return pltpu.make_async_remote_copy(
            src_ref=raw.at[slot, :],
            dst_ref=raw.at[slot, :],
            send_sem=pass_send.at[d],
            recv_sem=pass_recv.at[d],
            device_id=sibling,
            device_id_type=MESH,
        )

    @pl.loop(1, half)
    def _(d):
        raw_copy(d).start()

    pass_copy(0).start()

    def sl(i):
        return slice(i * NB, (i + 1) * NB)

    def wait_tile(i):
        if i >= per_dev:
            @pl.when(r == 0)
            def _():
                tile_copy(i, 1, 0).wait_recv()
                for k in range(per_dev):
                    tile[sl(i), sl(k)] = tile[sl(k), sl(i)].T

        @pl.when((r != i // per_dev) & ((r != 0) | (i < per_dev)))
        def _():
            tile_copy(i, 1).wait_recv()

        @pl.when(r == i // per_dev)
        def _():
            tile_in(i).wait()

    zero = rows[pl.ds(pl.multiple_of(r * ch, ch), SUB), 0:NB] * 0.0
    inverses = []
    for j in range(blocks):
        if j == 0:
            wait_tile(0)
        inv = lower_inverse(tile[sl(j), sl(j)], zero)
        inverses.append(inv)
        if j == 0:
            for i in range(1, blocks):
                wait_tile(i)
            for d in range(1, n_row):
                rows_copy(d).wait_recv()
        if j == min(1, blocks - 1):
            @pl.loop(1, half)
            def _(d):
                raw_copy(d).wait_recv()
                pass_copy(d).start()

        solved = dot_nt(rows[:, sl(j)], inv)
        rows[:, sl(j)] = solved
        if j + 1 < blocks:
            lower = dot_nt(tile[(j + 1) * NB :, sl(j)], inv)
            tile[(j + 1) * NB :, sl(j)] = lower
            for k in range(j + 1, blocks):
                at = (k - j - 1) * NB
                pivot = lower[at : at + NB, :]
                tile[k * NB :, sl(k)] = tile[k * NB :, sl(k)] - dot_nt(lower[at:, :], pivot)
                rows[:, sl(k)] = rows[:, sl(k)] - dot_nt(solved, pivot)

    factor_ref[...] = rows[own_rows, :]
    weights = [None] * blocks
    for j in reversed(range(blocks)):
        value = rows[:, sl(j)]
        for i in range(j + 1, blocks):
            value = value - dot_nn(weights[i], tile[sl(i), sl(j)])
        weights[j] = dot_nn(value, inverses[j])
    weight = jnp.concatenate([w.astype(BF16) for w in weights], axis=1)

    @pl.loop(0, half)
    def _(d):
        pass_copy(d).wait_recv()

    trail_in.wait()
    wide = trailing_ref.shape[1]
    step = min(512, wide)
    for s in range(0, wide, step):
        term = lax.dot_general(
            weight, raw[s : s + step, :], (((1,), (1,)), ((), ())), preferred_element_type=F32
        )
        updated_ref[:, s : s + step] = (
            trail[:, s : s + step].astype(F32) - term
        ).astype(BF16)

    for i in range(blocks):
        @pl.when(r == i // per_dev)
        def _():
            for d in range(1, n_row):
                tile_copy(i, d, (i // per_dev + d) % n_row).wait_send()
    for d in range(1, n_row):
        rows_copy(d).wait_send()

    @pl.loop(1, half)
    def _(d):
        raw_copy(d).wait_send()

    @pl.loop(0, half)
    def _(d):
        pass_copy(d).wait_send()


def per_device(n_row, n_col, diagonal_tile, panel, trailing):
    order = diagonal_tile.shape[1]
    ch = panel.shape[0]
    dma = pltpu.SemaphoreType.DMA
    vmem = pl.BlockSpec(memory_space=pltpu.VMEM)
    return pl.pallas_call(
        functools.partial(kernel, n_row, n_col),
        out_shape=(
            jax.ShapeDtypeStruct(panel.shape, F32),
            jax.ShapeDtypeStruct(trailing.shape, BF16),
        ),
        in_specs=[pl.BlockSpec(memory_space=pltpu.HBM)] * 3,
        out_specs=(vmem, vmem),
        scratch_shapes=[
            pltpu.VMEM((order, order), F32),
            pltpu.VMEM((n_row * ch, order), F32),
            pltpu.VMEM((n_col * ch, order), BF16),
            pltpu.VMEM(trailing.shape, BF16),
            dma((order // NB,)),
            dma,
            dma,
            dma((order // NB, n_row - 1)),
            dma((order // NB,)),
            dma((n_row - 1,)),
            dma((n_row - 1,)),
            dma((n_col // 2 - 1,)),
            dma((n_col // 2 - 1,)),
            dma((n_col // 2,)),
            dma((n_col // 2,)),
        ],
        compiler_params=pltpu.CompilerParams(
            collective_id=0, has_side_effects=True, vmem_limit_bytes=67_000_000
        ),
    )(diagonal_tile, panel, trailing)


def solution(mesh):
    return jax.shard_map(
        functools.partial(per_device, mesh.shape["row"], mesh.shape["col"]),
        mesh=mesh,
        in_specs=(P("row", None), P(("row", "col"), None), P("col", "row")),
        out_specs=(P(("row", "col"), None), P("col", "row")),
        check_vma=False,
    )
```

```python
import functools

import jax
import jax.numpy as jnp
from jax import lax
from jax.experimental import pallas as pl
from jax.experimental.pallas import tpu as pltpu
from jax.sharding import PartitionSpec as P

F32 = jnp.float32
BF16 = jnp.bfloat16
NB = 128
SUB = 8
BASE = 32
MESH = pl.DeviceIdType.MESH


def split2(x):
    hi = x.astype(BF16)
    return hi, (x - hi.astype(F32)).astype(BF16)


def dot3(a, b, dims):
    dims = (dims, ((), ()))
    a_hi, a_lo = split2(a)
    b_hi, b_lo = split2(b)
    dot = functools.partial(lax.dot_general, dimension_numbers=dims, preferred_element_type=F32)
    return dot(a_hi, b_hi) + (dot(a_hi, b_lo) + dot(a_lo, b_hi))


def dot_nt(a, b):
    return dot3(a, b, ((1,), (1,)))


def dot_nn(a, b):
    return dot3(a, b, ((1,), (0,)))


def row_of(x, s):
    return jnp.broadcast_to(x[s : s + 1, :], x.shape)


def lower_inverse(a, zero):
    halves = BASE // SUB
    eye = (
        lax.broadcasted_iota(jnp.int32, (NB, NB), 0) == lax.broadcasted_iota(jnp.int32, (NB, NB), 1)
    ).astype(F32)
    iota = lax.broadcasted_iota(jnp.int32, (SUB, NB), 0)
    chunks = [(a[s : s + BASE, :], eye[s : s + BASE, :]) for s in range(0, NB, BASE)]
    inverse_rows = []
    for kb in range(NB // BASE):
        cur = [
            [part[h * SUB : (h + 1) * SUB, :] for part in chunks[kb]] for h in range(halves)
        ]
        first = kb * BASE
        last = kb + 1 == NB // BASE
        parts = (1,) if last else (0, 1)
        cols = [
            {
                h: jnp.broadcast_to(cur[h][0][:, first + c : first + c + 1], (SUB, NB)) + zero
                for h in range(c // SUB, halves)
            }
            for c in range(BASE)
        ]
        scale = [jnp.zeros((SUB, NB), F32) for _ in range(halves)]
        pivot = row_of(cols[0][0], 0)
        for k in range(BASE):
            hk, sk = k // SUB, k % SUB
            root = lax.rsqrt(pivot)
            scale[hk] = jnp.where(iota == sk, root, scale[hk])
            if k + 1 < BASE:
                hn, sn = (k + 1) // SUB, (k + 1) % SUB
                ahead = root * row_of(cols[k][hn], sn)
                pivot = row_of(cols[k + 1][hn], sn) - ahead * ahead
            inv = root * root
            mult = {h: cols[k][h] * inv for h in range(hk, halves)}
            mult[hk] = jnp.where(iota > sk, mult[hk], 0.0)
            for c in range(k + 1, BASE):
                row = row_of(cols[k][c // SUB], c % SUB)
                for h in range(c // SUB, halves):
                    cols[c][h] = cols[c][h] - mult[h] * row
            for part in parts:
                row = row_of(cur[hk][part], sk)
                for h in range(hk, halves):
                    cur[h][part] = cur[h][part] - mult[h] * row
        done = [
            jnp.concatenate([cur[h][part] * scale[h] for h in range(halves)], axis=0)
            for part in range(2)
        ]
        inverse_rows.append(done[1])
        if not last:
            pieces = []
            for part in range(2):
                hi = done[part].astype(BF16).astype(F32)
                pieces.append((hi, done[part] - hi))
            left = jnp.concatenate([pieces[0][0], pieces[0][0], pieces[0][1]], axis=0)
            left = left.T.astype(BF16)
            right = jnp.concatenate(
                [jnp.concatenate([hi, lo, hi], axis=0) for hi, lo in pieces], axis=1
            ).astype(BF16)
            start = (kb + 1) * BASE
            change = lax.dot_general(
                left[start:, :], right, (((1,), (0,)), ((), ())), preferred_element_type=F32
            )
            for j in range(kb + 1, NB // BASE):
                at = j * BASE - start
                chunks[j] = tuple(
                    chunks[j][part] - change[at : at + BASE, part * NB : (part + 1) * NB]
                    for part in range(2)
                )
    return jnp.concatenate(inverse_rows, axis=0)


def kernel(
    n_row, n_col,
    tile_ref, panel_ref, trailing_ref,
    factor_ref, updated_ref,
    tile, rows, raw, trail, full,
    tile_local, panel_local, trail_local,
    tile_send, tile_recv, rows_send, rows_recv, raw_send, raw_recv, pass_send, pass_recv,
):
    r = lax.axis_index("row")
    c = lax.axis_index("col")
    order = tile_ref.shape[1]
    blocks = order // NB
    per_dev = tile_ref.shape[0] // NB
    ch = panel_ref.shape[0]

    def row_peer(d):
        return (lax.rem(r + d, n_row), c)

    half = n_col // 2
    sibling = (r, c + 1 - 2 * lax.rem(c, 2))

    def col_peer(d):
        return (r, lax.rem(c + 2 * d, n_col))

    barrier = pltpu.get_barrier_semaphore()
    for d in range(1, n_row):
        pl.semaphore_signal(barrier, inc=1, device_id=row_peer(d), device_id_type=MESH)

    pl.semaphore_signal(barrier, inc=1, device_id=sibling, device_id_type=MESH)

    @pl.loop(1, half)
    def _(d):
        pl.semaphore_signal(barrier, inc=1, device_id=col_peer(d), device_id_type=MESH)

    own_raw = pl.ds(pl.multiple_of(c * ch, ch), ch)
    own_rows = pl.ds(pl.multiple_of(r * ch, ch), ch)
    panel_in = pltpu.make_async_copy(panel_ref, rows.at[own_rows, :], panel_local)
    panel_in.start()

    def tile_in(i):
        return pltpu.make_async_copy(
            tile_ref.at[pl.ds((i % per_dev) * NB, NB), :],
            tile.at[pl.ds(i * NB, NB), :],
            tile_local.at[i],
        )

    for i in range(blocks):
        @pl.when(r == i // per_dev)
        def _():
            tile_in(i).start()

    trail_in = pltpu.make_async_copy(trailing_ref, trail, trail_local)
    trail_in.start()
    panel_in.wait()
    raw[own_raw, :] = rows[own_rows, :].astype(BF16)
    pl.semaphore_wait(barrier, n_row - 1 + half)

    def tile_copy(i, d, target=None):
        source = pl.ds((i % per_dev) * NB, NB)
        left = per_dev if target == 0 else 0
        cols = pl.ds(left * NB, (i + 1 - left) * NB)
        return pltpu.make_async_remote_copy(
            src_ref=tile_ref.at[source, cols],
            dst_ref=tile.at[pl.ds(i * NB, NB), cols],
            send_sem=tile_send.at[i, d - 1],
            recv_sem=tile_recv.at[i],
            device_id=row_peer(d),
            device_id_type=MESH,
        )

    def rows_copy(d):
        return pltpu.make_async_remote_copy(
            src_ref=panel_ref,
            dst_ref=rows.at[own_rows, :],
            send_sem=rows_send.at[d - 1],
            recv_sem=rows_recv.at[d - 1],
            device_id=row_peer(d),
            device_id_type=MESH,
        )

    def raw_copy(d):
        return pltpu.make_async_remote_copy(
            src_ref=raw.at[own_raw, :],
            dst_ref=raw.at[own_raw, :],
            send_sem=raw_send.at[d - 1],
            recv_sem=raw_recv.at[d - 1],
            device_id=col_peer(d),
            device_id_type=MESH,
        )

    for i in range(blocks):
        @pl.when(r == i // per_dev)
        def _():
            for d in range(1, n_row):
                tile_copy(i, d, (i // per_dev + d) % n_row).start()

    for d in range(1, n_row):
        rows_copy(d).start()

    def pass_copy(d):
        slot = pl.ds(pl.multiple_of(lax.rem(c + n_col - 2 * d, n_col) * ch, ch), ch)
        return pltpu.make_async_remote_copy(
            src_ref=raw.at[slot, :],
            dst_ref=raw.at[slot, :],
            send_sem=pass_send.at[d],
            recv_sem=pass_recv.at[d],
            device_id=sibling,
            device_id_type=MESH,
        )

    @pl.loop(1, half)
    def _(d):
        raw_copy(d).start()

    pass_copy(0).start()

    def sl(i):
        return slice(i * NB, (i + 1) * NB)

    def wait_tile(i):
        if i >= per_dev:
            @pl.when(r == 0)
            def _():
                tile_copy(i, 1, 0).wait_recv()
                for k in range(per_dev):
                    tile[sl(i), sl(k)] = tile[sl(k), sl(i)].T

        @pl.when((r != i // per_dev) & ((r != 0) | (i < per_dev)))
        def _():
            tile_copy(i, 1).wait_recv()

        @pl.when(r == i // per_dev)
        def _():
            tile_in(i).wait()

    zero = rows[pl.ds(pl.multiple_of(r * ch, ch), SUB), 0:NB] * 0.0
    full[...] = jnp.zeros_like(full)
    weights = [None] * blocks
    for j in range(blocks):
        if j == 0:
            wait_tile(0)
        done = j * NB
        coupling = dot_nn(tile[sl(j), :done], full[:done, :done]) if j else None
        inv = lower_inverse(tile[sl(j), sl(j)], zero)
        if j == 0:
            for i in range(1, blocks):
                wait_tile(i)
            for d in range(1, n_row):
                rows_copy(d).wait_recv()
        if j == min(1, blocks - 1):
            @pl.loop(1, half)
            def _(d):
                raw_copy(d).wait_recv()
                pass_copy(d).start()

        solved = dot_nt(rows[:, sl(j)], inv)
        rows[:, sl(j)] = solved
        inverse_row = inv
        if j:
            inverse_row = jnp.concatenate([-dot_nn(inv, coupling), inv], axis=1)
        full[sl(j), : done + NB] = inverse_row
        term = dot_nn(solved, inverse_row)
        for k in range(j + 1):
            weights[k] = term[:, sl(k)] if k == j else weights[k] + term[:, sl(k)]
        if j + 1 < blocks:
            lower = dot_nt(tile[(j + 1) * NB :, sl(j)], inv)
            tile[(j + 1) * NB :, sl(j)] = lower
            for k in range(j + 1, blocks):
                at = (k - j - 1) * NB
                pivot = lower[at : at + NB, :]
                tile[k * NB :, sl(k)] = tile[k * NB :, sl(k)] - dot_nt(lower[at:, :], pivot)
                rows[:, sl(k)] = rows[:, sl(k)] - dot_nt(solved, pivot)

    factor_ref[...] = rows[own_rows, :]
    weight = jnp.concatenate([w.astype(BF16) for w in weights], axis=1)

    @pl.loop(0, half)
    def _(d):
        pass_copy(d).wait_recv()

    trail_in.wait()
    wide = trailing_ref.shape[1]
    step = min(512, wide)
    for s in range(0, wide, step):
        term = lax.dot_general(
            weight, raw[s : s + step, :], (((1,), (1,)), ((), ())), preferred_element_type=F32
        )
        updated_ref[:, s : s + step] = (
            trail[:, s : s + step].astype(F32) - term
        ).astype(BF16)

    for i in range(blocks):
        @pl.when(r == i // per_dev)
        def _():
            for d in range(1, n_row):
                tile_copy(i, d, (i // per_dev + d) % n_row).wait_send()
    for d in range(1, n_row):
        rows_copy(d).wait_send()

    @pl.loop(1, half)
    def _(d):
        raw_copy(d).wait_send()

    @pl.loop(0, half)
    def _(d):
        pass_copy(d).wait_send()


def per_device(n_row, n_col, diagonal_tile, panel, trailing):
    order = diagonal_tile.shape[1]
    ch = panel.shape[0]
    dma = pltpu.SemaphoreType.DMA
    vmem = pl.BlockSpec(memory_space=pltpu.VMEM)
    return pl.pallas_call(
        functools.partial(kernel, n_row, n_col),
        out_shape=(
            jax.ShapeDtypeStruct(panel.shape, F32),
            jax.ShapeDtypeStruct(trailing.shape, BF16),
        ),
        in_specs=[pl.BlockSpec(memory_space=pltpu.HBM)] * 3,
        out_specs=(vmem, vmem),
        scratch_shapes=[
            pltpu.VMEM((order, order), F32),
            pltpu.VMEM((n_row * ch, order), F32),
            pltpu.VMEM((n_col * ch, order), BF16),
            pltpu.VMEM(trailing.shape, BF16),
            pltpu.VMEM((order, order), F32),
            dma((order // NB,)),
            dma,
            dma,
            dma((order // NB, n_row - 1)),
            dma((order // NB,)),
            dma((n_row - 1,)),
            dma((n_row - 1,)),
            dma((n_col // 2 - 1,)),
            dma((n_col // 2 - 1,)),
            dma((n_col // 2,)),
            dma((n_col // 2,)),
        ],
        compiler_params=pltpu.CompilerParams(
            collective_id=0, has_side_effects=True, vmem_limit_bytes=67_000_000
        ),
    )(diagonal_tile, panel, trailing)


def solution(mesh):
    return jax.shard_map(
        functools.partial(per_device, mesh.shape["row"], mesh.shape["col"]),
        mesh=mesh,
        in_specs=(P("row", None), P(("row", "col"), None), P("col", "row")),
        out_specs=(P(("row", "col"), None), P("col", "row")),
        check_vma=False,
    )
```
